128 devices in a mesh: member: 16 (over x_hi, z, core), fsdp: 8 (over y, x_lo).
Axes of the slice: x: 4 (x_hi: 2, x_lo: 2; x = x_hi * 2 + x_lo), y: 4, z: 4, core: 2. Of those that a mesh axis runs over, the one named last changes fastest.
Arguments:
- attn_queries: bfloat16 [16, 1024, 16, 128], P('member', 'fsdp'), may hold values from -27 to 27
- attn_keys: bfloat16 [16, 1024, 16, 128], P('member', 'fsdp'), may hold values from -7.5 to 7.5
- attn_values: bfloat16 [16, 1024, 16, 128], P('member', 'fsdp'), may hold values from -6 to 6
- out_grad: bfloat16 [16, 1024, 4096], P('member', 'fsdp'), may hold values from -6 to 6
- out_proj: bfloat16 [16, 4096, 2048], P('member', 'fsdp'), may hold values from -0.125 to 0.125
- first_moment: float32 [16, 4096, 2048], P('member', 'fsdp'), may hold values from -4 to 4
- second_moment: float32 [16, 4096, 2048], P('member', 'fsdp'), may hold values from 0.05 to 5
- explore_noise: bfloat16 [16, 4096, 2048], P('member', 'fsdp'), may hold values from -0.4375 to 0.4375
- donor_index: int32 [16], replicated, may hold values from 0 to 15, as said below
- copy_flag: int32 [16], replicated, may hold values from 0 to 1, as said below
Outputs:
- new_proj: bfloat16 [16, 4096, 2048], P('member', 'fsdp')
- new_first: float32 [16, 4096, 2048], P('member', 'fsdp')
- new_second: float32 [16, 4096, 2048], P('member', 'fsdp')
The draws below stay inside these ranges and needn't reach their ends.
Inputs may be any that keep to these rules, and one draw needn't show every extreme that they name: `donor_index`: every entry names one of the same four members (which four may differ from call to call); none of those four has copy_flag 1. `copy_flag`: exactly 4 entries are 1.
All inputs are finite; a program needn't handle non-finite values.
Results may differ from the reference program's by a relative error of at most 0.017.
Values may be sent and summed in bfloat16 or wider, within the bound.
No kernel may reach another device: no remote copies, remote signals or barrier semaphores. Data moves between devices by JAX's collectives and lax.ppermute only.
A program may use at most 128 MiB of HBM per device.

```python
import math
import jax
import jax.numpy as jnp
from jax import lax

D = 4096
HEAD_DIM = 128
HEADS = 16
TOK_DEV = 128
SEQ = 1024
HID = 2048
MEMBERS = 16
N_FSDP = 8


def drawn_pair(key):
    base = jax.random.fold_in(key, 29)
    key_query, key_key = jax.random.split(base, 2)
    shape = (MEMBERS, SEQ, HEADS, HEAD_DIM)
    queries = jnp.clip(jax.random.normal(key_query, shape, jnp.float32), -4.0, 4.0)
    keys = jnp.clip(jax.random.normal(key_key, shape, jnp.float32), -4.0, 4.0)
    return (queries, keys)


def draw_attn_queries(key, part):
    return drawn_pair(key)[0].astype(jnp.bfloat16)


def draw_attn_keys(key, part):
    return drawn_pair(key)[1].astype(jnp.bfloat16)


def pairing(key):
    base = jax.random.fold_in(key, 41)
    key_order, key_pick = jax.random.split(base, 2)
    middle = (jax.random.permutation(key_order, MEMBERS - 2) + 1).astype(jnp.int32)
    ends = jnp.array([0, MEMBERS - 1], jnp.int32)
    order = jnp.concatenate([ends, middle]).astype(jnp.int32)
    quarter = MEMBERS // 4
    picked = jax.random.randint(key_pick, (MEMBERS,), 0, quarter).astype(jnp.int32)
    picked = picked.at[order[MEMBERS - 1]].set(0).at[order[MEMBERS - 2]].set(1)
    donors = order[picked]
    flags = jnp.zeros((MEMBERS,), jnp.int32).at[order[MEMBERS - quarter:]].set(1)
    return (donors, flags)


def draw_donor_index(key, part):
    return pairing(key)[0]


def draw_copy_flag(key, part):
    return pairing(key)[1]


def with_spikes(result, rng, source, target, blocks, factor):
    owner, partner = [(jnp.arange(result.shape[dim]) // (result.shape[dim] // blocks)).reshape([-1 if axis == dim else 1 for axis in range(result.ndim)]) for dim in (source, target)]
    chosen = jax.random.permutation(rng, blocks)[partner]
    strong = (owner == chosen) | (owner == (partner + blocks // 2) % blocks)
    return jnp.where(strong, factor * result, result)


def block_scale(rng, extent, pieces, low, top_value):
    level, own = 1.0, jax.random.fold_in(rng, 6)
    for dim, shards_of in pieces:
        draws = jnp.exp(jax.random.uniform(jax.random.fold_in(own, dim), (shards_of,), jnp.float32, low / len(pieces), top_value / len(pieces)))
        level = level * jnp.repeat(draws, extent[dim] // shards_of).reshape([-1 if axis == dim else 1 for axis in range(len(extent))])
    return level


def bell_draw(own_key, extent, spread, bound, pieces=(), kind=jnp.bfloat16):
    loudness = block_scale(own_key, extent, pieces, -0.22, 0.18) if pieces else 1.0
    entries = jax.random.normal(own_key, extent, jnp.float32) * spread * loudness
    return jnp.minimum(jnp.maximum(entries, -bound), bound).astype(kind)


def gaussian_with(own_key, shape, scale, reach, cuts, heavy, held_as=jnp.bfloat16):
    values = scale * jax.random.normal(own_key, shape, jnp.float32)
    if cuts:
        values = values * block_scale(own_key, shape, cuts, -0.22, 0.18)
    return jnp.clip(with_spikes(values, jax.random.fold_in(own_key, 3), *heavy), -reach, reach).astype(held_as)


def setup_inputs(seed: int = 0) -> dict:
    splits = jax.random.split(jax.random.key(seed), 11)
    attn_queries = draw_attn_queries(jax.random.fold_in(splits[10], 71), 0)
    attn_keys = draw_attn_keys(jax.random.fold_in(splits[10], 71), 0)
    attn_values = bell_draw(splits[2], (MEMBERS, SEQ, HEADS, HEAD_DIM), 1.0, 6.0, ((0, 16), (1, 8)))
    out_grad = gaussian_with(splits[3], (MEMBERS, SEQ, D), 1.0, 6.0, ((0, 16), (1, 8)), (1, 2, 8, 2.0))
    out_proj = bell_draw(splits[4], (MEMBERS, D, HID), HID ** -0.5, 0.125, ((0, 16), (1, 8)))
    first_moment = bell_draw(splits[5], (MEMBERS, D, HID), 0.5, 4.0, ((0, 16), (1, 8)), jnp.float32)
    second_moment = jnp.clip(jnp.exp(math.log(5.0) - 4.6051702 * jax.random.uniform(splits[6], (MEMBERS, D, HID), jnp.float32) ** block_scale(splits[6], (MEMBERS, D, HID), ((0, 16), (1, 8)), -0.2, 0.2)), 0.05, 5.0)
    explore_noise = bell_draw(splits[7], (MEMBERS, D, HID), 0.03, 0.4375, ((0, 16), (1, 8)))
    donor_index = draw_donor_index(jax.random.fold_in(splits[10], 71), 0)
    copy_flag = draw_copy_flag(jax.random.fold_in(splits[10], 71), 0)
    return dict(attn_queries=attn_queries, attn_keys=attn_keys, attn_values=attn_values, out_grad=out_grad, out_proj=out_proj, first_moment=first_moment, second_moment=second_moment, explore_noise=explore_noise, donor_index=donor_index, copy_flag=copy_flag)


masked_value = -1e+30
beta_first = 0.9
beta_second = 0.95
learn_rate = 0.001
decay_rate = 0.1
epsilon = 1e-08

def member_context(queries, keys, values):
    sequence = queries.shape[0]
    scores = jnp.einsum('qhe,khe->hqk', queries.astype(jnp.float32), keys.astype(jnp.float32)) * HEAD_DIM ** (-0.5)
    position = jnp.arange(sequence, dtype=jnp.int32)
    allowed = position[:, None] >= position[None, :]
    scores = jnp.where(allowed[None], scores, masked_value)
    maximum = lax.optimization_barrier(jnp.max(scores, axis=-1, keepdims=True))
    weights = jnp.where(allowed[None], jnp.exp(scores - maximum), jnp.float32(0.0))
    totals = lax.optimization_barrier(jnp.sum(weights, axis=-1))
    rounded = weights.astype(jnp.bfloat16)
    context = jnp.einsum('hqk,khe->qhe', rounded.astype(jnp.float32), values.astype(jnp.float32))
    context = context / jnp.transpose(totals)[:, :, None]
    return context.astype(jnp.bfloat16).reshape(sequence, HEADS * HEAD_DIM)

def member_step(items):
    queries, keys, values, grad_out, weight, first, second = items
    context = member_context(queries, keys, values)
    blocks = (context.reshape(N_FSDP, TOK_DEV, HEADS * HEAD_DIM), grad_out.reshape(N_FSDP, TOK_DEV, D))

    def add_block(running, pair):
        context_rows, grad_rows = pair
        partial_sum = jnp.dot(grad_rows.T, context_rows, preferred_element_type=jnp.float32)
        partial_sum = lax.optimization_barrier(partial_sum.astype(jnp.bfloat16)).astype(jnp.float32)
        return (running + partial_sum, None)
    gradient, unused = lax.scan(add_block, jnp.zeros((D, HEADS * HEAD_DIM), jnp.float32), blocks)
    moment_one = beta_first * first + (1.0 - beta_first) * gradient
    moment_two = beta_second * second + (1.0 - beta_second) * gradient * gradient
    bias_first = 1.0 - beta_first ** 100.0
    bias_second = 1.0 - beta_second ** 100.0
    step_size = moment_one / bias_first / (jnp.sqrt(moment_two / bias_second) + epsilon)
    weight_float = weight.astype(jnp.float32)
    updated = (weight_float - learn_rate * (step_size + decay_rate * weight_float)).astype(jnp.bfloat16)
    return (updated, moment_one, moment_two)

def reference(attn_queries, attn_keys, attn_values, out_grad, out_proj, first_moment, second_moment, explore_noise, donor_index, copy_flag):
    updated, moment_one, moment_two = lax.map(member_step, (attn_queries, attn_keys, attn_values, out_grad, out_proj, first_moment, second_moment))
    source = jnp.where(copy_flag == 1, donor_index, jnp.arange(MEMBERS, dtype=jnp.int32)).astype(jnp.int32)
    chosen = jnp.take(updated, source, axis=0)
    new_first = jnp.take(moment_one, source, axis=0)
    new_second = jnp.take(moment_two, source, axis=0)
    flagged = (copy_flag == 1)[:, None, None]
    perturbed = (chosen.astype(jnp.float32) + explore_noise.astype(jnp.float32)).astype(jnp.bfloat16)
    new_proj = jnp.where(flagged, perturbed, chosen)
    return (new_proj, new_first, new_second)
```

```python
import functools

import jax
import jax.numpy as jnp
from jax import lax
from jax.experimental import pallas as pl
from jax.experimental.pallas import tpu as pltpu
from jax.sharding import Mesh
from jax.sharding import PartitionSpec as P

CHIP = ("xh", "z")
FSDP = ("y", "xl")
CHIPS = 8
CORES = 2
GROUPS = 8
bf16 = jnp.bfloat16
f32 = jnp.float32

beta_first = 0.9
beta_second = 0.95
learn_rate = 0.001
decay_rate = 0.1
epsilon = 1e-08


DONOR, SERVED, FLAG, REST, CORE = 8, 9, 10, 11, 12


def plan_kernel(donor_ref, flag_ref, done_ref, place_ref, table_ref, served_ref, used_ref, source_ref):
    members = CHIPS * CORES
    me, core = place_ref[0], place_ref[1]
    for m in range(members):
        used_ref[m] = 0
    for q in range(CHIPS):
        first = jnp.logical_and(flag_ref[2 * q] == 1, done_ref[2 * q] == 0)
        second = jnp.logical_and(flag_ref[2 * q + 1] == 1, done_ref[2 * q + 1] == 0)
        need = jnp.logical_or(first, second)
        source = jnp.where(first, donor_ref[2 * q], donor_ref[2 * q + 1])
        source = jnp.where(need, source, 2 * q)
        source_ref[q] = source
        table_ref[q] = source // 2

        @pl.when(need)
        def _(source=source):
            used_ref[source] = 1

    rest = jnp.int32(0)
    for m in range(members):
        donor = donor_ref[m]
        chip = donor // 2
        lead = jnp.where(used_ref[2 * chip] == 1, 2 * chip, 2 * chip + 1)
        wants = jnp.logical_and(flag_ref[m] == 1, done_ref[m] == 0)
        served = jnp.logical_and(wants, jnp.logical_and(donor == lead, donor == source_ref[m // 2]))
        served = served.astype(jnp.int32)
        used_ref[members + m] = served
        served_ref[m] = done_ref[m] | served
        rest = rest + wants.astype(jnp.int32) - served
    mine = me // 2
    lead = jnp.where(used_ref[2 * mine] == 1, 2 * mine, 2 * mine + 1)
    table_ref[DONOR] = (lead == me).astype(jnp.int32)
    table_ref[SERVED] = used_ref[members + me]
    table_ref[FLAG] = flag_ref[me]
    table_ref[REST] = rest
    table_ref[CORE] = core


def make_plan(donor_index, copy_flag, done, place):
    smem = pl.BlockSpec(memory_space=pltpu.SMEM)
    return pl.pallas_call(
        plan_kernel,
        in_specs=[smem] * 4,
        out_specs=[smem] * 2,
        out_shape=[jax.ShapeDtypeStruct((16,), jnp.int32), jax.ShapeDtypeStruct((16,), jnp.int32)],
        scratch_shapes=[pltpu.SMEM((32,), jnp.int32), pltpu.SMEM((8,), jnp.int32)],
        name="plan",
    )(donor_index, copy_flag, done, place)


def pack_kernel(table_ref, weight_ref, first_ref, second_ref, keep_ref, send_ref):
    own = pl.program_id(0) == table_ref[CORE]
    width = weight_ref.shape[-1]

    def fill(ref):
        ref[:, :width] = weight_ref[...]
        ref[:, width : 2 * width] = first_ref[...].astype(bf16)
        ref[:, 2 * width :] = second_ref[...].astype(bf16)

    @pl.when(own)
    def _():
        fill(keep_ref)

    @pl.when(jnp.logical_not(own))
    def _():
        fill(send_ref)


def held(mine, other):
    def index(h, p, table_ref):
        wanted = table_ref[CORE] if mine else 1 - table_ref[CORE]
        return jnp.where(h == wanted, p, jnp.where(h < wanted, 0, CHIPS - 1)), 0, 0

    del other
    return index


def pack_halves(table, weight, first, second):
    rows, width = weight.shape
    block = rows // (CORES * CHIPS)
    spec = pl.BlockSpec((block, width), lambda h, p, t: (h * CHIPS + p, 0))
    shape = jax.ShapeDtypeStruct((CHIPS, block, 3 * width), bf16)
    return pl.pallas_call(
        pack_kernel,
        grid_spec=pltpu.PrefetchScalarGridSpec(
            num_scalar_prefetch=1,
            grid=(CORES, CHIPS),
            in_specs=[spec, spec, spec],
            out_specs=[
                pl.BlockSpec((None, block, 3 * width), held(True, None)),
                pl.BlockSpec((None, block, 3 * width), held(False, None)),
            ],
        ),
        out_shape=[shape, shape],
        name="pack",
    )(table, weight, first, second)


def swap_cores(array):
    return lax.ppermute(array, "c", [(0, 1), (1, 0)])


def spread(table, keep, send):
    other = swap_cores(send)
    half = jnp.where(table[DONOR] == 1, keep, other)
    return lax.all_to_all(half, CHIP, 0, 0, tiled=True)


def choose_kernel(table_ref, in_ref, out_ref):
    out_ref[...] = in_ref[...]


def collect(table, slices):
    _, block, width = slices.shape
    chosen = pl.pallas_call(
        choose_kernel,
        grid_spec=pltpu.PrefetchScalarGridSpec(
            num_scalar_prefetch=1,
            grid=(CHIPS,),
            in_specs=[pl.BlockSpec((1, block, width), lambda q, t: (t[q], 0, 0))],
            out_specs=pl.BlockSpec((1, block, width), lambda q, t: (q, 0, 0)),
        ),
        out_shape=jax.ShapeDtypeStruct(slices.shape, slices.dtype),
        name="choose",
    )(table, slices)
    near = lax.all_to_all(chosen, CHIP, 0, 0, tiled=True)
    return near, swap_cores(near)


def attention_kernel(own_ref, *refs):
    blocks, order_ref, out_ref = refs[: GROUPS - 1], refs[GROUPS - 1], refs[GROUPS]
    heads = refs[GROUPS + 1]
    token_count, size = own_ref.shape[2:]
    for number, block in enumerate((own_ref,) + blocks):
        at = pl.multiple_of(order_ref[number] * token_count, token_count)
        for kind in range(3):
            for head in range(2):
                heads[kind, head, pl.ds(at, token_count), :] = block[kind, head]
    rows = 256
    sequence = GROUPS * token_count
    diagonal = lax.broadcasted_iota(jnp.int32, (rows, rows), 0) >= lax.broadcasted_iota(
        jnp.int32, (rows, rows), 1
    )
    for head in range(2):
        for start in range(0, sequence, rows):
            end = start + rows
            query = heads[0, head, start:end, :]
            scores = lax.dot_general(
                query, heads[1, head, :end, :], (((1,), (1,)), ((), ())), preferred_element_type=f32
            ) * (size ** (-0.5))
            last = jnp.where(diagonal, scores[:, start:], -1e30)
            scores = last if start == 0 else jnp.concatenate([scores[:, :start], last], axis=1)
            maximum = jnp.max(scores, axis=1, keepdims=True)
            weights = jnp.exp(scores - maximum)
            total = jnp.sum(weights, axis=1, keepdims=True)
            context = jnp.dot(
                weights.astype(bf16), heads[2, head, :end, :], preferred_element_type=f32
            )
            out_ref[start:end, head * size : (head + 1) * size] = (context / total).astype(bf16)


def attention(blocks, order):
    token_count, size = blocks[0].shape[2:]
    sequence = GROUPS * token_count
    vmem = pl.BlockSpec(memory_space=pltpu.VMEM)
    return pl.pallas_call(
        attention_kernel,
        in_specs=[vmem] * GROUPS + [pl.BlockSpec(memory_space=pltpu.SMEM)],
        out_specs=vmem,
        out_shape=jax.ShapeDtypeStruct((sequence, 2 * size), bf16),
        scratch_shapes=[pltpu.VMEM((3, 2, sequence, size), bf16)],
        name="attention",
    )(*blocks, order)


def update_kernel(
    table_ref, order_ref, *refs
):
    contexts = refs[:GROUPS]
    columns_ref, weight_ref, first_ref, second_ref, noise_ref, near_ref, far_ref = refs[GROUPS : GROUPS + 7]
    proj_out, first_out, second_out, gradient = refs[GROUPS + 7 :]
    half, piece = pl.program_id(0), pl.program_id(1)
    rows, width = weight_ref.shape
    group_width = width // GROUPS

    @pl.when(jnp.logical_and(half == 0, piece == 0))
    def _():
        for number in range(GROUPS):
            gradient[order_ref[number]] = lax.dot_general(
                columns_ref[...], contexts[number][...], (((0,), (0,)), ((), ())), preferred_element_type=f32
            )

    served = table_ref[SERVED] == 1
    at = pl.multiple_of((half * CHIPS + piece) * rows, rows)

    def update(weight_of, first_of, second_of, noisy):
        for number in range(GROUPS):
            lanes = slice(number * group_width, (number + 1) * group_width)
            slope = gradient[number, pl.ds(at, rows), :]
            moment_one = beta_first * first_of(lanes) + (1.0 - beta_first) * slope
            moment_two = beta_second * second_of(lanes) + (1.0 - beta_second) * slope * slope
            step = (moment_one * (1.0 / (1.0 - beta_first**100.0))) / (
                jnp.sqrt(moment_two * (1.0 / (1.0 - beta_second**100.0))) + epsilon
            )
            weight = weight_of(lanes)
            updated = (weight - learn_rate * (step + decay_rate * weight)).astype(bf16)
            if noisy:
                updated = (updated.astype(f32) + noise_ref[:, lanes].astype(f32)).astype(bf16)
            proj_out[:, lanes] = updated
            first_out[:, lanes] = moment_one
            second_out[:, lanes] = moment_two

    def from_packed(ref):
        def part(offset):
            return lambda lanes: ref[:, offset + lanes.start : offset + lanes.stop].astype(f32)

        update(part(0), part(width), part(2 * width), True)

    @pl.when(jnp.logical_not(served))
    def _():
        update(
            lambda lanes: weight_ref[:, lanes].astype(f32),
            lambda lanes: first_ref[:, lanes],
            lambda lanes: second_ref[:, lanes],
            False,
        )

    @pl.when(jnp.logical_and(served, half == table_ref[CORE]))
    def _():
        from_packed(near_ref)

    @pl.when(jnp.logical_and(served, half != table_ref[CORE]))
    def _():
        from_packed(far_ref)


def update_step(table, order, contexts, columns, weight, first, second, noise, near, far):
    rows, width = weight.shape
    block = rows // (CORES * CHIPS)
    sequence = columns.shape[0]
    group_width = width // GROUPS
    row_spec = pl.BlockSpec((block, width), lambda h, p, t, o: (h * CHIPS + p, 0))
    whole = lambda shape: pl.BlockSpec(shape, lambda h, p, t, o: (0, 0), pipeline_mode=pl.Buffered(1))
    near_index, far_index = held(True, None), held(False, None)
    return pl.pallas_call(
        update_kernel,
        grid_spec=pltpu.PrefetchScalarGridSpec(
            num_scalar_prefetch=2,
            grid=(CORES, CHIPS),
            in_specs=[whole((sequence, group_width))] * GROUPS
            + [whole((sequence, rows))]
            + [row_spec] * 4
            + [
                pl.BlockSpec((None, block, 3 * width), lambda h, p, t, o: near_index(h, p, t)),
                pl.BlockSpec((None, block, 3 * width), lambda h, p, t, o: far_index(h, p, t)),
            ],
            out_specs=[row_spec] * 3,
            scratch_shapes=[pltpu.VMEM((GROUPS, rows, group_width), f32)],
        ),
        out_shape=[
            jax.ShapeDtypeStruct((rows, width), bf16),
            jax.ShapeDtypeStruct((rows, width), f32),
            jax.ShapeDtypeStruct((rows, width), f32),
        ],
        compiler_params=pltpu.CompilerParams(vmem_limit_bytes=50 << 20),
        name="update",
    )(table, order, *contexts, columns, weight, first, second, noise, near, far)


def exchange_blocks(pieces, me):
    received = [lax.dynamic_index_in_dim(pieces, me, 0, keepdims=False)]
    for shift in range(1, GROUPS):
        block = lax.dynamic_index_in_dim(pieces, me ^ shift, 0, keepdims=False)
        received.append(lax.ppermute(block, FSDP, [(i, i ^ shift) for i in range(GROUPS)]))
    return received


def gather_ring(own):
    count = lax.axis_size("y")
    right = [(i, (i + 1) % count) for i in range(count)]
    left = [(i, (i - 1) % count) for i in range(count)]
    half = own.shape[0] // 2
    partner = lax.ppermute(own, "xl", [(0, 1), (1, 0)])
    found = {}
    for side, block in ((0, own), (1, partner)):
        found[0, side] = block
        found[-1, side] = lax.ppermute(block, "y", right)
        found[1, side] = lax.ppermute(block, "y", left)
    for side in (0, 1):
        upper = lax.ppermute(found[-1, side][:half], "y", right)
        lower = lax.ppermute(found[1, side][half:], "y", left)
        found[2, side] = jnp.concatenate([upper, lower], axis=0)
    return found


def body(queries, keys, values, out_grad, out_proj, first_moment, second_moment, noise, donor_index, copy_flag):
    token_count, head_count, head_size = queries.shape[1:]
    width = head_count * head_size
    row_count = out_proj.shape[1]
    per_group = head_count // GROUPS
    group_width = per_group * head_size
    sequence = token_count * GROUPS
    core = lax.axis_index("c")
    y, xl = lax.axis_index("y"), lax.axis_index("xl")
    me = y * 2 + xl
    member = lax.axis_index(CHIP) * 2 + core
    place = jnp.stack([member, core]).astype(jnp.int32)

    qkv = jnp.stack([queries[0], keys[0], values[0]])
    qkv = qkv.reshape(3, token_count, GROUPS, per_group, head_size).transpose(2, 0, 3, 1, 4)
    blocks = exchange_blocks(qkv, me)

    table, done = make_plan(donor_index, copy_flag, jnp.zeros((16,), jnp.int32), place)
    keep, send = pack_halves(table, out_proj[0], first_moment[0], second_moment[0])
    state = spread(table, keep, send)

    grads = out_grad[0].reshape(token_count, GROUPS, row_count).transpose(1, 0, 2)
    grad_blocks = exchange_blocks(grads, me)

    order = me ^ lax.iota(jnp.int32, GROUPS)
    context = attention(blocks, order)
    stacked = jnp.stack(grad_blocks)
    columns = jnp.take(stacked, order, axis=0).reshape(sequence, row_count)

    bundle = jnp.concatenate([context, columns], axis=1).reshape(
        CORES, CHIPS, sequence // (CORES * CHIPS), group_width + row_count
    )
    slices = spread(
        table,
        lax.dynamic_index_in_dim(bundle, core, 0, keepdims=False),
        lax.dynamic_index_in_dim(bundle, 1 - core, 0, keepdims=False),
    )
    near, far = collect(table, slices)
    taken = jnp.stack([jnp.where(core == 0, near, far), jnp.where(core == 0, far, near)])
    bundle = jnp.where(table[SERVED] == 1, taken, bundle).reshape(sequence, group_width + row_count)
    context, columns = bundle[:, :group_width], bundle[:, group_width:]

    found = gather_ring(context)
    places = [(0, 0), (0, 1), (-1, 0), (-1, 1), (1, 0), (1, 1), (2, 0), (2, 1)]
    context_order = jnp.stack([((y + dy) % 4) * 2 + (xl ^ side) for dy, side in places]).astype(jnp.int32)

    state_near, state_far = collect(table, state)
    outputs = update_step(
        table,
        context_order,
        [found[p] for p in places],
        columns,
        out_proj[0],
        first_moment[0],
        second_moment[0],
        noise[0],
        state_near,
        state_far,
    )

    def unserved(carry):
        return carry[0] > 0

    def serve(carry):
        _, done, proj, first, second = carry
        table, done = make_plan(donor_index, copy_flag, done, place)
        keep, send = pack_halves(table, proj, first, second)
        near, far = collect(table, spread(table, keep, send))
        taken = jnp.stack([jnp.where(core == 0, near, far), jnp.where(core == 0, far, near)])
        taken = taken.reshape(row_count, 3 * width)
        served = table[SERVED] == 1
        perturbed = (taken[:, :width].astype(f32) + noise[0].astype(f32)).astype(bf16)
        return (
            table[REST],
            done,
            jnp.where(served, perturbed, proj),
            jnp.where(served, taken[:, width : 2 * width].astype(f32), first),
            jnp.where(served, taken[:, 2 * width :].astype(f32), second),
        )

    _, _, proj, first, second = lax.while_loop(unserved, serve, (table[REST], done, *outputs))
    return proj[None], first[None], second[None]


def solution(mesh):
    finer = Mesh(mesh.devices.reshape(2, 4, 2, 4, 2), ("xh", "z", "c", "y", "xl"))
    member = ("xh", "z", "c")
    four = P(member, FSDP, None, None)
    three = P(member, FSDP, None)
    in_specs = (four, four, four, three, three, three, three, three, P(), P())
    return jax.shard_map(body, mesh=finer, in_specs=in_specs, out_specs=(three, three, three), check_vma=False)
```

```python
import functools

import jax
import jax.numpy as jnp
from jax import lax
from jax.experimental import pallas as pl
from jax.experimental.pallas import tpu as pltpu
from jax.sharding import Mesh
from jax.sharding import PartitionSpec as P


CHIP = ("xh", "z")
FSDP = ("y", "xl")
CHIPS = 8
CORES = 2
GROUPS = 8
bf16 = jnp.bfloat16
f32 = jnp.float32

beta_first = 0.9
beta_second = 0.95
learn_rate = 0.001
decay_rate = 0.1
epsilon = 1e-08


DONOR, SERVED, REST, CORE = 8, 9, 10, 11
EXCHANGE, RING = 16, 24
PLACES = [(0, 0), (0, 1), (-1, 0), (-1, 1), (1, 0), (1, 1), (2, 0), (2, 1)]
STEPS = 4


def plan_kernel(donor_ref, flag_ref, done_ref, place_ref, table_ref, served_ref, used_ref, source_ref):
    members = CHIPS * CORES
    me, core, y, xl = place_ref[0], place_ref[1], place_ref[2], place_ref[3]
    for s in range(GROUPS):
        table_ref[EXCHANGE + s] = (y * 2 + xl) ^ s
    for s, (step, side) in enumerate(PLACES):
        table_ref[RING + s] = ((y + step) & 3) * 2 + (xl ^ side)
    for m in range(members):
        used_ref[m] = 0
    for q in range(CHIPS):
        first = jnp.logical_and(flag_ref[2 * q] == 1, done_ref[2 * q] == 0)
        second = jnp.logical_and(flag_ref[2 * q + 1] == 1, done_ref[2 * q + 1] == 0)
        need = jnp.logical_or(first, second)
        source = jnp.where(first, donor_ref[2 * q], donor_ref[2 * q + 1])
        source = jnp.where(need, source, 2 * q)
        source_ref[q] = source
        table_ref[q] = source // 2

        @pl.when(need)
        def _(source=source):
            used_ref[source] = 1

    rest = jnp.int32(0)
    for m in range(members):
        donor = donor_ref[m]
        chip = donor // 2
        lead = jnp.where(used_ref[2 * chip] == 1, 2 * chip, 2 * chip + 1)
        wants = jnp.logical_and(flag_ref[m] == 1, done_ref[m] == 0)
        served = jnp.logical_and(wants, jnp.logical_and(donor == lead, donor == source_ref[m // 2]))
        served = served.astype(jnp.int32)
        used_ref[members + m] = served
        served_ref[m] = done_ref[m] | served
        rest = rest + wants.astype(jnp.int32) - served
    mine = me // 2
    lead = jnp.where(used_ref[2 * mine] == 1, 2 * mine, 2 * mine + 1)
    table_ref[DONOR] = (lead == me).astype(jnp.int32)
    table_ref[SERVED] = used_ref[members + me]
    table_ref[REST] = rest
    table_ref[CORE] = core


def make_plan(donor_index, copy_flag, done, place):
    smem = pl.BlockSpec(memory_space=pltpu.SMEM)
    return pl.pallas_call(
        plan_kernel,
        in_specs=[smem] * 4,
        out_specs=[smem] * 2,
        out_shape=[jax.ShapeDtypeStruct((32,), jnp.int32), jax.ShapeDtypeStruct((16,), jnp.int32)],
        scratch_shapes=[pltpu.SMEM((32,), jnp.int32), pltpu.SMEM((8,), jnp.int32)],
        name="plan",
    )(donor_index, copy_flag, done, place)


def held(mine, last):
    def index(h, p, table_ref):
        wanted = table_ref[CORE] if mine else 1 - table_ref[CORE]
        return jnp.where(h == wanted, p, jnp.where(h < wanted, 0, last))

    return index


def pack_kernel(table_ref, weight_ref, first_ref, second_ref, keep_ref, send_ref):
    own = pl.program_id(0) == table_ref[CORE]
    width = weight_ref.shape[-1]

    def fill(ref):
        ref[:, :width] = weight_ref[...]
        ref[:, width : 2 * width] = first_ref[...].astype(bf16)
        ref[:, 2 * width :] = second_ref[...].astype(bf16)

    @pl.when(own)
    def _():
        fill(keep_ref)

    @pl.when(jnp.logical_not(own))
    def _():
        fill(send_ref)


def pack_halves(table, weight, first, second):
    rows, width = weight.shape
    block = rows // (CORES * STEPS)
    spec = pl.BlockSpec((block, width), lambda h, p, t: (h * STEPS + p, 0))
    mine, other = held(True, STEPS - 1), held(False, STEPS - 1)
    shape = jax.ShapeDtypeStruct((rows // CORES, 3 * width), bf16)
    return pl.pallas_call(
        pack_kernel,
        grid_spec=pltpu.PrefetchScalarGridSpec(
            num_scalar_prefetch=1,
            grid=(CORES, STEPS),
            in_specs=[spec, spec, spec],
            out_specs=[
                pl.BlockSpec((block, 3 * width), lambda h, p, t: (mine(h, p, t), 0)),
                pl.BlockSpec((block, 3 * width), lambda h, p, t: (other(h, p, t), 0)),
            ],
        ),
        out_shape=[shape, shape],
        name="pack",
    )(table, weight, first, second)


SMEM_SPEC = pl.BlockSpec(memory_space=pltpu.SMEM)
ANY_SPEC = pl.BlockSpec(memory_space=pl.ANY)


def copier(kernel, table, inputs, shapes, copies):
    return pl.pallas_call(
        kernel,
        in_specs=[SMEM_SPEC] + [ANY_SPEC] * len(inputs),
        out_specs=[ANY_SPEC] * len(shapes),
        out_shape=shapes,
        scratch_shapes=[pltpu.SemaphoreType.DMA((copies,))],
    )(table, *inputs)


def finish(started):
    for copy in started:
        copy.wait()


def either(condition, true_ref, false_ref, out_ref, semaphore):
    @pl.when(condition)
    def _():
        pltpu.make_async_copy(true_ref, out_ref, semaphore).start()

    @pl.when(jnp.logical_not(condition))
    def _():
        pltpu.make_async_copy(false_ref, out_ref, semaphore).start()

    return pltpu.make_async_copy(true_ref, out_ref, semaphore)


def pick_kernel(table_ref, keep_ref, other_ref, out_ref, semaphores):
    donor = table_ref[DONOR] == 1
    rows = keep_ref.shape[0] // CHIPS
    finish(
        [
            either(
                donor,
                keep_ref.at[pl.ds(rows * n, rows)],
                other_ref.at[pl.ds(rows * n, rows)],
                out_ref.at[pl.ds(rows * n, rows)],
                semaphores.at[n],
            )
            for n in range(CHIPS)
        ]
    )


def swap_cores(array):
    return lax.ppermute(array, "c", [(0, 1), (1, 0)])


def pick(table, keep, send):
    shape = [jax.ShapeDtypeStruct(keep.shape, keep.dtype)]
    return copier(pick_kernel, table, (keep, swap_cores(send)), shape, CHIPS)[0]


def chip_exchange(half):
    rows, width = half.shape
    pieces = half.reshape(CHIPS, rows // CHIPS, width)
    pieces = lax.all_to_all(pieces, CHIP, 0, 0, tiled=True)
    return pieces.reshape(rows, width)


def choose_kernel(table_ref, in_ref, out_ref, semaphores):
    rows = in_ref.shape[0] // CHIPS
    started = []
    for q in range(CHIPS):
        at = pl.multiple_of(table_ref[q] * rows, rows)
        copy = pltpu.make_async_copy(
            in_ref.at[pl.ds(at, rows)], out_ref.at[pl.ds(q * rows, rows)], semaphores.at[q]
        )
        copy.start()
        started.append(copy)
    finish(started)


def choose(table, slices):
    shape = [jax.ShapeDtypeStruct(slices.shape, slices.dtype)]
    return copier(choose_kernel, table, (slices,), shape, CHIPS)[0]


def arrange_kernel(table_ref, grad_ref, *refs):
    outs, semaphores = refs[:GROUPS], refs[GROUPS]
    width = grad_ref.shape[1] // GROUPS
    started = []
    for n in range(GROUPS):
        at = pl.multiple_of(table_ref[EXCHANGE + n] * width, width)
        copy = pltpu.make_async_copy(grad_ref.at[:, pl.ds(at, width)], outs[n], semaphores.at[n])
        copy.start()
        started.append(copy)
    finish(started)


def bundle_kernel(table_ref, context_ref, *refs):
    blocks, (keep_ref, send_ref, semaphores) = refs[:GROUPS], refs[GROUPS:]
    core = table_ref[CORE]
    half, inner = keep_ref.shape[0], context_ref.shape[1]
    tokens, width = blocks[0].shape
    started = []
    for n, (ref, part) in enumerate(((keep_ref, core), (send_ref, 1 - core))):
        copy = pltpu.make_async_copy(
            context_ref.at[pl.ds(pl.multiple_of(part * half, half), half)],
            ref.at[:, pl.ds(0, inner)],
            semaphores.at[GROUPS + n],
        )
        copy.start()
        started.append(copy)
    for n in range(GROUPS):
        source = table_ref[EXCHANGE + n]
        at = pl.multiple_of((source % (GROUPS // 2)) * tokens, tokens)
        kept = source // (GROUPS // 2) == core
        keep_at = keep_ref.at[pl.ds(at, tokens), pl.ds(inner, width)]
        send_at = send_ref.at[pl.ds(at, tokens), pl.ds(inner, width)]

        @pl.when(kept)
        def _(n=n, keep_at=keep_at):
            pltpu.make_async_copy(blocks[n], keep_at, semaphores.at[n]).start()

        @pl.when(jnp.logical_not(kept))
        def _(n=n, send_at=send_at):
            pltpu.make_async_copy(blocks[n], send_at, semaphores.at[n]).start()

        started.append(pltpu.make_async_copy(blocks[n], keep_at, semaphores.at[n]))
    finish(started)


def merge_kernel(table_ref, keep_ref, send_ref, near_ref, far_ref, context_ref, columns_ref, semaphores):
    served = table_ref[SERVED] == 1
    half, inner = keep_ref.shape[0], context_ref.shape[1]
    width = columns_ref.shape[1]
    started = []
    for n, (taken, own) in enumerate(((near_ref, keep_ref), (far_ref, send_ref))):
        for k, (out, at, size) in enumerate(((context_ref, 0, inner), (columns_ref, inner, width))):
            started.append(
                either(
                    served,
                    taken.at[:, pl.ds(at, size)],
                    own.at[:, pl.ds(at, size)],
                    out.at[pl.ds(n * half, half)],
                    semaphores.at[2 * n + k],
                )
            )
    finish(started)


def attention_kernel(own_ref, *refs):
    blocks, table_ref, out_ref = refs[: GROUPS - 1], refs[GROUPS - 1], refs[GROUPS]
    heads = refs[GROUPS + 1]
    token_count, size = own_ref.shape[2:]
    for number, block in enumerate((own_ref,) + blocks):
        at = pl.multiple_of(table_ref[EXCHANGE + number] * token_count, token_count)
        for kind in range(3):
            for head in range(2):
                heads[kind, head, pl.ds(at, token_count), :] = block[kind, head]
    rows = 256
    sequence = GROUPS * token_count
    diagonal = lax.broadcasted_iota(jnp.int32, (rows, rows), 0) >= lax.broadcasted_iota(
        jnp.int32, (rows, rows), 1
    )
    for head in range(2):
        for start in range(0, sequence, rows):
            end = start + rows
            query = heads[0, head, start:end, :]
            scores = lax.dot_general(
                query, heads[1, head, :end, :], (((1,), (1,)), ((), ())), preferred_element_type=f32
            ) * (size ** (-0.5))
            last = jnp.where(diagonal, scores[:, start:], -1e30)
            scores = last if start == 0 else jnp.concatenate([scores[:, :start], last], axis=1)
            maximum = jnp.max(scores, axis=1, keepdims=True)
            weights = jnp.exp(scores - maximum)
            total = jnp.sum(weights, axis=1, keepdims=True)
            context = jnp.dot(
                weights.astype(bf16), heads[2, head, :end, :], preferred_element_type=f32
            )
            out_ref[start:end, head * size : (head + 1) * size] = (context / total).astype(bf16)


def attention(blocks, table):
    token_count, size = blocks[0].shape[2:]
    sequence = GROUPS * token_count
    vmem = pl.BlockSpec(memory_space=pltpu.VMEM)
    return pl.pallas_call(
        attention_kernel,
        in_specs=[vmem] * GROUPS + [pl.BlockSpec(memory_space=pltpu.SMEM)],
        out_specs=vmem,
        out_shape=jax.ShapeDtypeStruct((sequence, 2 * size), bf16),
        scratch_shapes=[pltpu.VMEM((3, 2, sequence, size), bf16)],
        name="attention",
    )(*blocks, table)


def update_kernel(table_ref, *refs, parts, fresh):
    contexts = (refs[:parts], refs[parts : 2 * parts])
    refs = refs[2 * parts :]
    columns_ref, weight_ref, first_ref, second_ref, noise_ref = refs[:5]
    near, far, outs = refs[5:8], refs[8:11], refs[11 if fresh else 14 :]
    proj_out, first_out, second_out, gradient = outs
    half, side = pl.program_id(0), pl.program_id(1)
    length = columns_ref.shape[0] // parts

    for number in range(2):

        @pl.when(side == number)
        def _(number=number):
            total = None
            for part in range(parts):
                product = lax.dot_general(
                    columns_ref[part * length : (part + 1) * length, :],
                    contexts[number][part][...],
                    (((0,), (0,)), ((), ())),
                    preferred_element_type=f32,
                )
                total = product if total is None else total + product
            gradient[...] = total

    rows = weight_ref.shape[0]
    served = table_ref[SERVED] == 1

    def update(weight_ref, first_ref, second_ref, noisy):
        for start in range(0, rows, 64):
            at = slice(start, start + 64)
            slope = gradient[at, :]
            moment_one = beta_first * first_ref[at, :].astype(f32) + (1.0 - beta_first) * slope
            moment_two = beta_second * second_ref[at, :].astype(f32) + (1.0 - beta_second) * slope * slope
            step = (moment_one * (1.0 / (1.0 - beta_first**100.0))) / (
                jnp.sqrt(moment_two * (1.0 / (1.0 - beta_second**100.0))) + epsilon
            )
            weight = weight_ref[at, :].astype(f32)
            updated = (weight - learn_rate * (step + decay_rate * weight)).astype(bf16)
            if noisy:
                updated = (updated.astype(f32) + noise_ref[at, :].astype(f32)).astype(bf16)
            proj_out[at, :] = updated
            first_out[at, :] = moment_one
            second_out[at, :] = moment_two

    @pl.when(jnp.logical_not(served))
    def _():
        update(weight_ref, first_ref, second_ref, False)

    @pl.when(jnp.logical_and(served, half == table_ref[CORE]))
    def _():
        update(*near, True)

    @pl.when(jnp.logical_and(served, half != table_ref[CORE]))
    def _():
        update(*far, True)


def update_piece(number, table, contexts, columns, weight, first, second, noise, near, far, outputs):
    parts = len(contexts[0])
    rows, width = weight.shape
    sequence = columns.shape[0]
    group_width = width // GROUPS
    block = rows // CORES
    mine, other = held(True, 1), held(False, 1)
    base = RING + 2 * number
    whole = pl.BlockSpec((sequence // parts, group_width), lambda h, j, t: (0, 0), pipeline_mode=pl.Buffered(1))
    piece = pl.BlockSpec((block, group_width), lambda h, j, t: (h, t[base + j]))

    def packed(index):
        return [
            pl.BlockSpec((block, group_width), lambda h, j, t, k=k: (0, k * GROUPS + t[base + index(h, j, t)]))
            for k in range(3)
        ]

    inputs = [*contexts[0], *contexts[1], columns, weight, first, second, noise, near, near, near, far, far, far]
    in_specs = (
        [whole] * (2 * parts)
        + [pl.BlockSpec((sequence, block), lambda h, j, t: (0, h))]
        + [piece] * 4
        + packed(mine)
        + packed(other)
    )
    aliases = {}
    if outputs is not None:
        aliases = {1 + len(inputs) + k: k for k in range(3)}
        inputs += outputs
        in_specs += [ANY_SPEC] * 3
    return pl.pallas_call(
        functools.partial(update_kernel, parts=parts, fresh=outputs is None),
        grid_spec=pltpu.PrefetchScalarGridSpec(
            num_scalar_prefetch=1,
            grid=(CORES, 2),
            in_specs=in_specs,
            out_specs=[piece] * 3,
            scratch_shapes=[pltpu.VMEM((block, group_width), f32)],
        ),
        out_shape=[
            jax.ShapeDtypeStruct((rows, width), bf16),
            jax.ShapeDtypeStruct((rows, width), f32),
            jax.ShapeDtypeStruct((rows, width), f32),
        ],
        input_output_aliases=aliases,
        name="update",
    )(table, *inputs)


def settle_kernel(table_ref, near_ref, far_ref, noise_ref, proj_ref, first_ref, second_ref, proj_out, first_out, second_out):
    served = table_ref[SERVED] == 1
    near = pl.program_id(0) == table_ref[CORE]
    width = proj_ref.shape[1]

    @pl.when(jnp.logical_not(served))
    def _():
        proj_out[...] = proj_ref[...]
        first_out[...] = first_ref[...]
        second_out[...] = second_ref[...]

    def take(ref):
        proj_out[...] = (ref[:, :width].astype(f32) + noise_ref[...].astype(f32)).astype(bf16)
        first_out[...] = ref[:, width : 2 * width].astype(f32)
        second_out[...] = ref[:, 2 * width :].astype(f32)

    @pl.when(jnp.logical_and(served, near))
    def _():
        take(near_ref)

    @pl.when(jnp.logical_and(served, jnp.logical_not(near)))
    def _():
        take(far_ref)


def settle(table, near, far, noise, outputs):
    rows, width = noise.shape
    block = rows // (CORES * STEPS)
    spec = pl.BlockSpec((block, width), lambda h, p, t: (h * STEPS + p, 0))
    mine, other = held(True, STEPS - 1), held(False, STEPS - 1)
    return pl.pallas_call(
        settle_kernel,
        grid_spec=pltpu.PrefetchScalarGridSpec(
            num_scalar_prefetch=1,
            grid=(CORES, STEPS),
            in_specs=[
                pl.BlockSpec((block, 3 * width), lambda h, p, t: (mine(h, p, t), 0)),
                pl.BlockSpec((block, 3 * width), lambda h, p, t: (other(h, p, t), 0)),
            ]
            + [spec] * 4,
            out_specs=[spec] * 3,
        ),
        out_shape=[jax.ShapeDtypeStruct(o.shape, o.dtype) for o in outputs],
        input_output_aliases={4: 0, 5: 1, 6: 2},
        name="settle",
    )(table, near, far, noise, *outputs)


def permute_blocks(blocks):
    return [blocks[0]] + [
        lax.ppermute(blocks[shift], FSDP, [(i, i ^ shift) for i in range(GROUPS)])
        for shift in range(1, GROUPS)
    ]


def gather_ring(own):
    count = lax.axis_size("y")
    right = [(i, (i + 1) % count) for i in range(count)]
    left = [(i, (i - 1) % count) for i in range(count)]
    half = own.shape[0] // 2
    partner = lax.ppermute(own, "xl", [(0, 1), (1, 0)])
    found = {}
    for side, block in ((0, own), (1, partner)):
        found[0, side] = [block]
        found[-1, side] = [lax.ppermute(block, "y", right)]
        found[1, side] = [lax.ppermute(block, "y", left)]
    for side in (0, 1):
        pieces = (found[-1, side][0][:half], right), (found[1, side][0][half:], left)
        found[2, side] = [lax.ppermute(piece, "y", way) for piece, way in pieces]
    return found


def body(queries, keys, values, out_grad, out_proj, first_moment, second_moment, noise, donor_index, copy_flag):
    token_count, head_count, head_size = queries.shape[1:]
    row_count = out_proj.shape[1]
    per_group = head_count // GROUPS
    group_width = per_group * head_size
    sequence = token_count * GROUPS
    core, y, xl = lax.axis_index("c"), lax.axis_index("y"), lax.axis_index("xl")
    me = y * 2 + xl
    member = lax.axis_index(CHIP) * 2 + core
    place = jnp.stack([member, core, y, xl]).astype(jnp.int32)
    weight, first, second, noise = out_proj[0], first_moment[0], second_moment[0], noise[0]

    table, done = make_plan(donor_index, copy_flag, jnp.zeros((16,), jnp.int32), place)
    keep, send = pack_halves(table, weight, first, second)
    state = chip_exchange(pick(table, keep, send))

    qkv = jnp.stack([queries[0], keys[0], values[0]])
    qkv = qkv.reshape(3, token_count, GROUPS, per_group, head_size).transpose(2, 0, 3, 1, 4)
    blocks = permute_blocks([lax.dynamic_index_in_dim(qkv, me ^ s, 0, keepdims=False) for s in range(GROUPS)])
    piece = jax.ShapeDtypeStruct((token_count, row_count), bf16)
    grad_blocks = permute_blocks(copier(arrange_kernel, table, (out_grad[0],), [piece] * GROUPS, GROUPS))

    context = attention(blocks, table)
    half = jax.ShapeDtypeStruct((sequence // 2, group_width + row_count), bf16)
    keep, send = copier(bundle_kernel, table, (context, *grad_blocks), [half, half], GROUPS + 2)
    picked, _ = lax.optimization_barrier((pick(table, keep, send), state))
    near = chip_exchange(choose(table, chip_exchange(picked)))
    far = swap_cores(near)
    shapes = [jax.ShapeDtypeStruct((sequence, n), bf16) for n in (group_width, row_count)]
    context, columns = copier(merge_kernel, table, (keep, send, near, far), shapes, 4)
    found = gather_ring(context)

    chosen, _ = lax.optimization_barrier((choose(table, state), near))
    state_near = chip_exchange(chosen)
    state_far = swap_cores(state_near)
    outputs = None
    for number in range(4):
        pair = [found[p] for p in PLACES[2 * number : 2 * number + 2]]
        outputs = update_piece(
            number, table, pair, columns, weight, first, second, noise, state_near, state_far, outputs
        )

    def unserved(carry):
        return carry[0] > 0

    def serve(carry):
        _, done, *outputs = carry
        table, done = make_plan(donor_index, copy_flag, done, place)
        keep, send = pack_halves(table, *outputs)
        near = chip_exchange(choose(table, chip_exchange(pick(table, keep, send))))
        outputs = settle(table, near, swap_cores(near), noise, outputs)
        return (table[REST], done, *outputs)

    _, _, proj, first, second = lax.while_loop(unserved, serve, (table[REST], done, *outputs))
    return proj[None], first[None], second[None]


def solution(mesh):
    finer = Mesh(mesh.devices.reshape(2, 4, 2, 4, 2), ("xh", "z", "c", "y", "xl"))
    member = ("xh", "z", "c")
    four = P(member, FSDP, None, None)
    three = P(member, FSDP, None)
    in_specs = (four, four, four, three, three, three, three, three, P(), P())

    return jax.shard_map(body, mesh=finer, in_specs=in_specs, out_specs=(three, three, three), check_vma=False)
```

```python
import functools

import jax
import jax.numpy as jnp
from jax import lax
from jax.experimental import pallas as pl
from jax.experimental.pallas import tpu as pltpu
from jax.sharding import Mesh
from jax.sharding import PartitionSpec as P


CHIP = ("xh", "z")
FSDP = ("y", "xl")
CHIPS = 8
CORES = 2
GROUPS = 8
bf16 = jnp.bfloat16
f32 = jnp.float32

beta_first = 0.9
beta_second = 0.95
learn_rate = 0.001
decay_rate = 0.1
epsilon = 1e-08


STEPS = 4
DONOR, SERVED, REST, CORE, FRESH = 8, 9, 10, 11, 12
EXCHANGE, RING, LEAD = 16, 24, 32
PLACES = [(0, 0), (-1, 0), (1, 0), (2, 0), (0, 1), (-1, 1), (1, 1), (2, 1)]


def plan_kernel(donor_ref, flag_ref, done_ref, lead_ref, place_ref, table_ref, served_ref, wanted_ref, source_ref):
    members = CHIPS * CORES
    me, core, y, xl = place_ref[0], place_ref[1], place_ref[2], place_ref[3]
    for s in range(GROUPS):
        table_ref[EXCHANGE + s] = (y * 2 + xl) ^ s
    for s, (step, side) in enumerate(PLACES):
        table_ref[RING + s] = ((y + step) & 3) * 2 + (xl ^ side)
    for m in range(members):
        wanted_ref[m] = 0
    for m in range(members):

        @pl.when(jnp.logical_and(flag_ref[m] == 1, done_ref[m] == 0))
        def _(m=m):
            wanted_ref[donor_ref[m]] = 1

    usable = jnp.int32(0)
    for q in range(CHIPS):
        lead = lead_ref[q]
        usable = usable | jnp.where(lead >= 0, wanted_ref[jnp.maximum(lead, 0)], 0)
    for q in range(CHIPS):
        chosen = jnp.where(wanted_ref[2 * q] == 1, 2 * q, 2 * q + 1)
        table_ref[LEAD + q] = jnp.where(usable == 1, lead_ref[q], chosen)
    table_ref[FRESH] = 1 - usable

    def can(m):
        lead = table_ref[LEAD + donor_ref[m] // 2]
        return jnp.logical_and(jnp.logical_and(flag_ref[m] == 1, done_ref[m] == 0), donor_ref[m] == lead)

    rest = jnp.int32(0)
    for q in range(CHIPS):
        first, second = can(2 * q), can(2 * q + 1)
        source = jnp.where(first, donor_ref[2 * q], jnp.where(second, donor_ref[2 * q + 1], 2 * q))
        table_ref[q] = source // 2
        for m, able in ((2 * q, first), (2 * q + 1, second)):
            served = jnp.logical_and(able, donor_ref[m] == source).astype(jnp.int32)
            source_ref[m] = served
            served_ref[m] = done_ref[m] | served
            wants = jnp.logical_and(flag_ref[m] == 1, done_ref[m] == 0).astype(jnp.int32)
            rest = rest + wants - served
    table_ref[DONOR] = (table_ref[LEAD + me // 2] == me).astype(jnp.int32)
    table_ref[SERVED] = source_ref[me]
    table_ref[REST] = rest
    table_ref[CORE] = core


def make_plan(donor_index, copy_flag, done, lead, place):
    smem = pl.BlockSpec(memory_space=pltpu.SMEM)
    return pl.pallas_call(
        plan_kernel,
        in_specs=[smem] * 5,
        out_specs=[smem] * 2,
        out_shape=[jax.ShapeDtypeStruct((40,), jnp.int32), jax.ShapeDtypeStruct((16,), jnp.int32)],
        scratch_shapes=[pltpu.SMEM((16,), jnp.int32), pltpu.SMEM((16,), jnp.int32)],
        name="plan",
    )(donor_index, copy_flag, done, lead, place)


def held(mine, last):
    def index(h, p, table_ref):
        wanted = table_ref[CORE] if mine else 1 - table_ref[CORE]
        return jnp.where(h == wanted, p, jnp.where(h < wanted, 0, last))

    return index


def pack_kernel(table_ref, weight_ref, first_ref, second_ref, keep_ref, send_ref):
    own = pl.program_id(0) == table_ref[CORE]
    width = weight_ref.shape[-1]

    def fill(ref):
        ref[:, :width] = weight_ref[...]
        ref[:, width : 2 * width] = first_ref[...].astype(bf16)
        ref[:, 2 * width :] = second_ref[...].astype(bf16)

    @pl.when(own)
    def _():
        fill(keep_ref)

    @pl.when(jnp.logical_not(own))
    def _():
        fill(send_ref)


def pack_halves(table, weight, first, second):
    rows, width = weight.shape
    block = rows // (CORES * STEPS)
    spec = pl.BlockSpec((block, width), lambda h, p, t: (h * STEPS + p, 0))
    mine, other = held(True, STEPS - 1), held(False, STEPS - 1)
    shape = jax.ShapeDtypeStruct((rows // CORES, 3 * width), bf16)
    return pl.pallas_call(
        pack_kernel,
        grid_spec=pltpu.PrefetchScalarGridSpec(
            num_scalar_prefetch=1,
            grid=(CORES, STEPS),
            in_specs=[spec, spec, spec],
            out_specs=[
                pl.BlockSpec((block, 3 * width), lambda h, p, t: (mine(h, p, t), 0)),
                pl.BlockSpec((block, 3 * width), lambda h, p, t: (other(h, p, t), 0)),
            ],
        ),
        out_shape=[shape, shape],
        name="pack",
    )(table, weight, first, second)


SMEM_SPEC = pl.BlockSpec(memory_space=pltpu.SMEM)
ANY_SPEC = pl.BlockSpec(memory_space=pl.ANY)
VMEM_SPEC = pl.BlockSpec(memory_space=pltpu.VMEM)


def copier(kernel, table, inputs, shapes, copies):
    return pl.pallas_call(
        kernel,
        in_specs=[SMEM_SPEC] + [VMEM_SPEC] * len(inputs),
        out_specs=[ANY_SPEC] * len(shapes),
        out_shape=shapes,
        scratch_shapes=[pltpu.SemaphoreType.DMA((copies,))],
    )(table, *inputs)


def finish(started):
    for copy in started:
        copy.wait()


def pick_kernel(table_ref, keep_ref, other_ref, out_ref, staged_ref, semaphores):
    donor = table_ref[DONOR] == 1
    rows = keep_ref.shape[0] // CHIPS
    parts = [pl.ds(rows * n, rows) for n in range(CHIPS)]
    for n, part in enumerate(parts):

        @pl.when(donor)
        def _(n=n, part=part):
            pltpu.make_async_copy(keep_ref.at[part], staged_ref.at[part], semaphores.at[n]).start()

        @pl.when(jnp.logical_not(donor))
        def _(n=n, part=part):
            pltpu.make_async_copy(other_ref.at[part], staged_ref.at[part], semaphores.at[n]).start()

    started = []
    for n, part in enumerate(parts):
        pltpu.make_async_copy(keep_ref.at[part], staged_ref.at[part], semaphores.at[n]).wait()
        copy = pltpu.make_async_copy(staged_ref.at[part], out_ref.at[part], semaphores.at[CHIPS + n])
        copy.start()
        started.append(copy)
    finish(started)


def swap_cores(array):
    return lax.ppermute(array, "c", [(0, 1), (1, 0)])


def pick(table, keep, send):
    return pl.pallas_call(
        pick_kernel,
        in_specs=[SMEM_SPEC, ANY_SPEC, ANY_SPEC],
        out_specs=ANY_SPEC,
        out_shape=jax.ShapeDtypeStruct(keep.shape, keep.dtype),
        scratch_shapes=[pltpu.VMEM(keep.shape, keep.dtype), pltpu.SemaphoreType.DMA((2 * CHIPS,))],
        name="pick",
    )(table, keep, swap_cores(send))


def chip_exchange(half):
    rows, width = half.shape
    pieces = half.reshape(CHIPS, rows // CHIPS, width)
    pieces = lax.all_to_all(pieces, CHIP, 0, 0, tiled=True)
    return pieces.reshape(rows, width)


def choose_kernel(table_ref, in_ref, out_ref, semaphores):
    rows = in_ref.shape[0] // CHIPS
    started = []
    for q in range(CHIPS):
        at = pl.multiple_of(table_ref[q] * rows, rows)
        copy = pltpu.make_async_copy(
            in_ref.at[pl.ds(at, rows)], out_ref.at[pl.ds(q * rows, rows)], semaphores.at[q]
        )
        copy.start()
        started.append(copy)
    finish(started)


def choose(table, slices):
    shape = [jax.ShapeDtypeStruct(slices.shape, slices.dtype)]
    return copier(choose_kernel, table, (slices,), shape, CHIPS)[0]


def stage_kernel(place_ref, query_ref, key_ref, value_ref, grad_ref, *refs):
    heads, grads, wide = refs[:GROUPS], refs[GROUPS : 2 * GROUPS], refs[2 * GROUPS]
    me = place_ref[2] * 2 + place_ref[3]
    tokens, head_count, size = query_ref.shape
    per_group = head_count // GROUPS
    width = grad_ref.shape[1] // GROUPS
    for kind, ref in enumerate((query_ref, key_ref, value_ref)):
        wide[...] = ref[...].astype(f32).reshape(tokens * head_count, size)
        for s in range(GROUPS):
            for head in range(per_group):
                start = (me ^ s) * per_group + head
                heads[s][kind, head] = wide[pl.ds(start, tokens, stride=head_count), :].astype(bf16)
    for s in range(GROUPS):
        at = pl.multiple_of((me ^ s) * width, width)
        grads[s][...] = grad_ref[:, pl.ds(at, width)]


def stage(place, queries, keys, values, grads):
    tokens, head_count, size = queries.shape
    head_block = jax.ShapeDtypeStruct((3, head_count // GROUPS, tokens, size), bf16)
    grad_block = jax.ShapeDtypeStruct((tokens, grads.shape[1] // GROUPS), bf16)
    outs = pl.pallas_call(
        stage_kernel,
        in_specs=[SMEM_SPEC] + [VMEM_SPEC] * 4,
        out_specs=[VMEM_SPEC] * (2 * GROUPS),
        out_shape=[head_block] * GROUPS + [grad_block] * GROUPS,
        scratch_shapes=[pltpu.VMEM((tokens * head_count, size), f32)],
        name="stage",
    )(place, queries, keys, values, grads)
    return outs[:GROUPS], outs[GROUPS:]


def turn_kernel(table_ref, *refs):
    blocks, out_ref = refs[:GROUPS], refs[GROUPS]
    tokens = blocks[0].shape[0]
    for n in range(GROUPS):
        at = pl.multiple_of(table_ref[EXCHANGE + n] * tokens, tokens)
        out_ref[:, pl.ds(at, tokens)] = blocks[n][...].T


def turn(table, blocks):
    tokens, rows = blocks[0].shape
    return pl.pallas_call(
        turn_kernel,
        in_specs=[SMEM_SPEC] + [VMEM_SPEC] * GROUPS,
        out_specs=VMEM_SPEC,
        out_shape=jax.ShapeDtypeStruct((rows, tokens * GROUPS), bf16),
        name="turn",
    )(table, *blocks)


def attention_kernel(own_ref, *refs):
    blocks, table_ref, out_ref = refs[: GROUPS - 1], refs[GROUPS - 1], refs[GROUPS]
    heads = refs[GROUPS + 1]
    token_count, size = own_ref.shape[2:]
    for number, block in enumerate((own_ref,) + blocks):
        at = pl.multiple_of(table_ref[EXCHANGE + number] * token_count, token_count)
        for kind in range(3):
            for head in range(2):
                heads[kind, head, pl.ds(at, token_count), :] = block[kind, head]
    rows = 256
    sequence = GROUPS * token_count
    diagonal = lax.broadcasted_iota(jnp.int32, (rows, rows), 0) >= lax.broadcasted_iota(
        jnp.int32, (rows, rows), 1
    )
    for head in range(2):
        for start in range(0, sequence, rows):
            end = start + rows
            query = heads[0, head, start:end, :]
            scores = lax.dot_general(
                query, heads[1, head, :end, :], (((1,), (1,)), ((), ())), preferred_element_type=f32
            ) * (size ** (-0.5))
            last = jnp.where(diagonal, scores[:, start:], -1e30)
            scores = last if start == 0 else jnp.concatenate([scores[:, :start], last], axis=1)
            maximum = jnp.max(scores, axis=1, keepdims=True)
            weights = jnp.exp(scores - maximum)
            total = jnp.sum(weights, axis=1, keepdims=True)
            context = jnp.dot(
                weights.astype(bf16), heads[2, head, :end, :], preferred_element_type=f32
            )
            out_ref[start:end, head * size : (head + 1) * size] = (context / total).astype(bf16)


def attention(blocks, table):
    token_count, size = blocks[0].shape[2:]
    sequence = GROUPS * token_count
    vmem = pl.BlockSpec(memory_space=pltpu.VMEM)
    return pl.pallas_call(
        attention_kernel,
        in_specs=[vmem] * GROUPS + [pl.BlockSpec(memory_space=pltpu.SMEM)],
        out_specs=vmem,
        out_shape=jax.ShapeDtypeStruct((sequence, 2 * size), bf16),
        scratch_shapes=[pltpu.VMEM((3, 2, sequence, size), bf16)],
        name="attention",
    )(*blocks, table)


def gradient_kernel(table_ref, *refs, parts):
    columns_ref, (out_ref, keep_ref, send_ref) = refs[sum(parts)], refs[-3:]
    half = keep_ref.shape[0]
    for number, count in enumerate(parts):
        context = refs[sum(parts[:number]) :][:count]

        @pl.when(pl.program_id(0) == number)
        def _(context=context):
            length = columns_ref.shape[1] // len(context)
            total = None
            for k, part in enumerate(context):
                product = jnp.dot(
                    columns_ref[:, k * length : (k + 1) * length], part[...], preferred_element_type=f32
                )
                total = product if total is None else total + product
            out_ref[...] = total

    for ref, part in ((keep_ref, table_ref[CORE]), (send_ref, 1 - table_ref[CORE])):
        ref[...] = out_ref[pl.ds(pl.multiple_of(part * half, half), half), :].astype(bf16)


def gradient_piece(start, table, contexts, columns, gradient):
    parts = tuple(len(context) for context in contexts)
    rows, _ = columns.shape
    group_width = contexts[0][0].shape[1]
    half = rows // CORES
    base = RING + start
    whole = lambda shape: pl.BlockSpec(shape, lambda j, t: (0, 0), pipeline_mode=pl.Buffered(1))
    inputs = [part for context in contexts for part in context] + [columns]
    in_specs = [whole(part.shape) for part in inputs]
    aliases = {}
    if gradient is not None:
        aliases = {1 + len(inputs) + k: k for k in range(3)}
        inputs += gradient
        in_specs += [ANY_SPEC] * 3
    out = lambda count: pl.BlockSpec((None, count, group_width), lambda j, t: (t[base + j], 0, 0))
    sizes = ((rows, f32), (half, bf16), (half, bf16))
    return pl.pallas_call(
        functools.partial(gradient_kernel, parts=parts),
        grid_spec=pltpu.PrefetchScalarGridSpec(
            num_scalar_prefetch=1,
            grid=(len(contexts),),
            in_specs=in_specs,
            out_specs=[out(count) for count, _ in sizes],
        ),
        out_shape=[jax.ShapeDtypeStruct((GROUPS, count, group_width), kind) for count, kind in sizes],
        input_output_aliases=aliases,
        name="gradient",
    )(table, *inputs)


def update_kernel(
    table_ref,
    gradient_ref,
    weight_ref,
    first_ref,
    second_ref,
    noise_ref,
    near_ref,
    far_ref,
    near_gradient_ref,
    far_gradient_ref,
    *refs,
):
    old, (proj_out, first_out, second_out) = refs[:-3], refs[-3:]
    served = table_ref[SERVED] == 1
    near = pl.program_id(0) == table_ref[CORE]
    width = noise_ref.shape[1]
    group_width = width // GROUPS

    def update(slopes, weight_of, first_of, second_of, noisy):
        for number in range(GROUPS):
            lanes = slice(number * group_width, (number + 1) * group_width)
            slope = slopes[number].astype(f32)
            moment_one = beta_first * first_of(lanes) + (1.0 - beta_first) * slope
            moment_two = beta_second * second_of(lanes) + (1.0 - beta_second) * slope * slope
            step = (moment_one * (1.0 / (1.0 - beta_first**100.0))) / (
                jnp.sqrt(moment_two * (1.0 / (1.0 - beta_second**100.0))) + epsilon
            )
            weight = weight_of(lanes)
            updated = (weight - learn_rate * (step + decay_rate * weight)).astype(bf16)
            if noisy:
                updated = (updated.astype(f32) + noise_ref[:, lanes].astype(f32)).astype(bf16)
            proj_out[:, lanes] = updated
            first_out[:, lanes] = moment_one
            second_out[:, lanes] = moment_two

    def taken(slopes, ref):
        def part(offset):
            return lambda lanes: ref[:, offset + lanes.start : offset + lanes.stop].astype(f32)

        update(slopes, part(0), part(width), part(2 * width), True)

    @pl.when(jnp.logical_not(served))
    def _():
        if old:
            for ref, out in zip(old, (proj_out, first_out, second_out)):
                out[...] = ref[...]
            return
        update(
            gradient_ref,
            lambda lanes: weight_ref[:, lanes].astype(f32),
            lambda lanes: first_ref[:, lanes],
            lambda lanes: second_ref[:, lanes],
            False,
        )

    @pl.when(jnp.logical_and(served, near))
    def _():
        taken(near_gradient_ref, near_ref)

    @pl.when(jnp.logical_and(served, jnp.logical_not(near)))
    def _():
        taken(far_gradient_ref, far_ref)


def update(table, gradient, weight, first, second, noise, near, far, near_gradient, far_gradient, old=()):
    rows, width = weight.shape
    steps = 4
    block = rows // (CORES * steps)
    mine, other = held(True, steps - 1), held(False, steps - 1)

    def own(h, p, t):
        return 0 if old else jnp.where(t[SERVED] == 1, 0, h * steps + p)

    def copied(h, p, t):
        return jnp.where(t[SERVED] == 1, h * steps + p, 0)

    def of_half(index):
        return lambda h, p, t: jnp.where(t[SERVED] == 1, index(h, p, t), 0)

    def rows_by(index, columns):
        return pl.BlockSpec((block, columns), lambda h, p, t: (index(h, p, t), 0))

    def groups_by(index):
        return pl.BlockSpec((GROUPS, block, width // GROUPS), lambda h, p, t: (0, index(h, p, t), 0))

    near_of, far_of = of_half(mine), of_half(other)
    spec = rows_by(copied if old else lambda h, p, t: h * steps + p, width)
    return pl.pallas_call(
        update_kernel,
        grid_spec=pltpu.PrefetchScalarGridSpec(
            num_scalar_prefetch=1,
            grid=(CORES, steps),
            in_specs=[groups_by(own)]
            + [rows_by(own, width)] * 3
            + [rows_by(copied, width), rows_by(near_of, 3 * width), rows_by(far_of, 3 * width)]
            + [groups_by(near_of), groups_by(far_of)]
            + [spec] * len(old),
            out_specs=[spec] * 3,
        ),
        out_shape=[
            jax.ShapeDtypeStruct((rows, width), bf16),
            jax.ShapeDtypeStruct((rows, width), f32),
            jax.ShapeDtypeStruct((rows, width), f32),
        ],
        input_output_aliases={10 + k: k for k in range(len(old))},
        name="update",
    )(table, gradient, weight, first, second, noise, near, far, near_gradient, far_gradient, *old)


def permute_blocks(blocks):
    return [blocks[0]] + [
        lax.ppermute(blocks[shift], FSDP, [(i, i ^ shift) for i in range(GROUPS)])
        for shift in range(1, GROUPS)
    ]


def gather_ring(own):
    count = lax.axis_size("y")
    right = [(i, (i + 1) % count) for i in range(count)]
    left = [(i, (i - 1) % count) for i in range(count)]
    half = own.shape[0] // 2
    partner = lax.ppermute(own, "xl", [(0, 1), (1, 0)])
    found = {}
    for side, block in ((0, own), (1, partner)):
        found[0, side] = [block]
        found[-1, side] = [lax.ppermute(block, "y", right)]
        found[1, side] = [lax.ppermute(block, "y", left)]
    for side in (0, 1):
        upper, lower = found[-1, side][0][:half], found[1, side][0][half:]
        found[2, side] = [lax.ppermute(upper, "y", right), lax.ppermute(lower, "y", left)]
    return found


def body(queries, keys, values, out_grad, out_proj, first_moment, second_moment, noise, donor_index, copy_flag):
    _, head_count, head_size = queries.shape[1:]
    row_count = out_proj.shape[1]
    per_group = head_count // GROUPS
    group_width = per_group * head_size
    core, y, xl = lax.axis_index("c"), lax.axis_index("y"), lax.axis_index("xl")
    member = lax.axis_index(CHIP) * 2 + core
    place = jnp.stack([member, core, y, xl]).astype(jnp.int32)
    weight, first, second, noise = out_proj[0], first_moment[0], second_moment[0], noise[0]

    head_blocks, grad_blocks = stage(place, queries[0], keys[0], values[0], out_grad[0])
    none = jnp.full((16,), -1, jnp.int32)
    table, done = make_plan(donor_index, copy_flag, jnp.zeros((16,), jnp.int32), none, place)
    state_keep, state_send = pack_halves(table, weight, first, second)
    state = chip_exchange(pick(table, state_keep, state_send))

    blocks = permute_blocks(head_blocks)
    grad_blocks = permute_blocks(grad_blocks)

    context = attention(blocks, table)
    found = gather_ring(context)
    state_near = chip_exchange(choose(table, state))
    state_far = swap_cores(state_near)

    columns = turn(table, grad_blocks)
    gradient = None
    for start, end in ((0, 4), (4, 7), (7, 8)):
        gradient = gradient_piece(start, table, [found[p] for p in PLACES[start:end]], columns, gradient)
    half = row_count // CORES
    gradient, keep, send = (
        array if array.dtype == f32 else array.reshape(GROUPS * half, group_width) for array in gradient
    )
    picked = pick(table, keep, send)
    picked, _ = lax.optimization_barrier((picked, state_near))
    slopes = chip_exchange(picked)
    near = chip_exchange(choose(table, slopes))

    def finished(table, near_state, far_state, near, old=()):
        pair = (array.reshape(GROUPS, half, group_width) for array in (near, swap_cores(near)))
        return update(table, gradient, weight, first, second, noise, near_state, far_state, *pair, old)

    outputs = finished(table, state_near, state_far, near)

    def unserved(carry):
        return carry[0][REST] > 0

    def serve(carry):
        table, done, slices, outputs = carry
        table, done = make_plan(donor_index, copy_flag, done, table[LEAD : LEAD + CHIPS], place)

        def again(slices):
            del slices
            return (chip_exchange(pick(table, state_keep, state_send)), chip_exchange(pick(table, keep, send)))

        slices = lax.cond(table[FRESH] == 1, again, lambda slices: slices, slices)
        near_state, near = (chip_exchange(choose(table, array)) for array in slices)
        return table, done, slices, finished(table, near_state, swap_cores(near_state), near, outputs)

    _, _, _, outputs = lax.while_loop(unserved, serve, (table, done, (state, slopes), outputs))
    proj, first, second = outputs
    return proj[None], first[None], second[None]


def solution(mesh):
    finer = Mesh(mesh.devices.reshape(2, 4, 2, 4, 2), ("xh", "z", "c", "y", "xl"))
    member = ("xh", "z", "c")
    four = P(member, FSDP, None, None)
    three = P(member, FSDP, None)
    in_specs = (four, four, four, three, three, three, three, three, P(), P())

    return jax.shard_map(body, mesh=finer, in_specs=in_specs, out_specs=(three, three, three), check_vma=False)
```
